512 devices in a mesh: section: 8 (over x, core), expert: 64 (over y, z).
Axes of the slice: x: 4, y: 8, z: 8, core: 2. Of those that a mesh axis runs over, the one named last changes fastest.
Arguments:
- carried: bfloat16 [8, 4096, 2048], P('section', 'expert'), may hold values from -6 to 6
- incoming: bfloat16 [1, 4096, 2048], P(None, 'expert'), may hold values from -6 to 6
- norm_gain: float32 [8, 2048], P('section'), may hold values from 0.25 to 1.75
- expert_ids: int32 [8, 2, 4096, 2], P('section', None, 'expert'), may hold values from 0 to 15, all different within a row; in each aligned block of 64 rows (0 to 63, 64 to 127, ..., all dimensions but the last counted through in order) at most 12 rows name the same one
- gate_weights: float32 [8, 2, 4096, 2], P('section', None, 'expert'), may hold values from 0.3 to 1
- w_gate: bfloat16 [8, 2048, 16384], P('section', None, 'expert'), may hold values from -0.125 to 0.125
- w_up: bfloat16 [8, 2048, 16384], P('section', None, 'expert'), may hold values from -0.125 to 0.125
- w_down: bfloat16 [8, 16384, 2048], P('section', 'expert'), may hold values from -0.1875 to 0.1875
Outputs:
- mixed: bfloat16 [8, 4096, 2048], P('section', 'expert')
The draws below stay inside these ranges and needn't reach their ends.
Inputs may be any that keep to these rules, and one draw needn't show every extreme that they name: `expert_ids`: in each aligned block of 64 rows (the tokens of one device for one section and step) every row names 2 different experts, and no expert is named by more than 12 rows; in some block some expert is named by exactly 12 rows.
All inputs are finite; a program needn't handle non-finite values.
Results may differ from the reference program's by a relative error of at most 0.007.
Values may be sent and summed in bfloat16 or wider, within the bound.
A program may use at most 64 MiB of HBM per device.

```python
import math
import jax
import jax.numpy as jnp
import numpy as np
from jax import lax

D = 2048
FF = 1024
EXPERTS = 16
TOP = 2
STEPS = 2
TOK_DEV = 64
SECTIONS = 8
TOKENS = 4096
SPLIT = 4
CAP = 12


def shard_levels(key, dims, shards, smallest, high):
    gain, own = 1.0, jax.random.fold_in(key, 6)
    for dim, blocks in shards:
        heights = jnp.exp(jax.random.uniform(jax.random.fold_in(own, dim), (blocks,), jnp.float32, smallest / len(shards), high / len(shards)))
        gain = gain * jnp.repeat(heights, dims[dim] // blocks).reshape([-1 if axis == dim else 1 for axis in range(len(dims))])
    return gain


def assign_block(stream_key, own, number, rows, count, top, reach, skew):
    sequence = jax.random.permutation(stream_key, count)
    packed, usual = portions_of(count, rows * top, reach, skew, True), portions_of(count, rows * top, reach, skew, False)
    places = jnp.arange(count)

    def named(tallies, turn):
        used = int((tallies > 0).sum())
        fixed = max(1, used // 4)
        shifted = fixed + (places - fixed + turn * (used - fixed)) % max(1, count - fixed)
        return jnp.zeros((count,), jnp.int32).at[sequence[jnp.where(places < fixed, places, shifted)]].set(jnp.asarray(tallies, jnp.int32))

    tallies = jnp.where(number % 4 == 0, named(packed, number // 4), named(usual, number - number // 4 - 1))
    mixed = jax.random.permutation(jax.random.fold_in(own, 3), count)
    donor, taker = mixed[0:count // 2 * 2:2], mixed[1:count // 2 * 2:2]
    slack = jnp.minimum(tallies[donor] - 1, reach - tallies[taker]) // 2
    slack = jnp.where((donor == sequence[0]) | (taker == sequence[0]) | (tallies[taker] == 0), 0, jnp.maximum(slack, 0))
    shifted = jax.random.randint(jax.random.fold_in(own, 4), (count // 2,), 0, 1 << 20) % (slack + 1)
    tallies = tallies.at[donor].add(-shifted).at[taker].add(shifted)
    members = jnp.searchsorted(jnp.cumsum(tallies), jnp.arange(rows * top), side="right").astype(jnp.int32)
    listing = members.reshape(top, rows).T
    listing = listing[jax.random.permutation(jax.random.fold_in(own, 1), rows)]
    turn = jax.random.randint(jax.random.fold_in(own, 2), (rows, 1), 0, top)
    return jnp.take_along_axis(listing, (jnp.arange(top)[None, :] + turn) % top, axis=1)


def portions_of(amount, total, reach, slope, full):
    loads = [(1 << 20) // math.isqrt(grade ** slope) + 1 for grade in range(1, amount + 1)]
    largest = reach if full else min(reach, max(-(-total // amount), total * loads[0] // sum(loads)))
    least = 1 if total - largest >= amount - 1 else 0
    counts, spare = [largest] + [least] * (amount - 1), total - largest - least * (amount - 1)
    while spare > 0:
        candidates = [i for i in range(1, amount) if counts[i] < largest] or [i for i in range(1, amount) if counts[i] < reach]
        whole, budget = sum([loads[i] for i in candidates]), spare
        for i in candidates:
            extra = min(reach - counts[i], max(1, budget * loads[i] // whole), spare)
            counts[i] = counts[i] + extra
            spare = spare - extra
    return np.array(counts)


def normal_values(key, shape, spread, most, split=(), held_as=jnp.bfloat16):
    result = jax.random.normal(key, shape, jnp.float32) * spread
    if len(split) > 0:
        result = shard_levels(key, shape, split, -0.22, 0.18) * result
    return jnp.clip(result, min=-most, max=most).astype(held_as)


def setup_inputs(seed: int = 0) -> dict:
    keys = jax.random.split(jax.random.key(seed), 9)
    carried = normal_values(keys[0], (SECTIONS, TOKENS, D), 1.0, 6.0, ((0, 8), (1, 64)))
    incoming = normal_values(keys[1], (STEPS - 1, TOKENS, D), 1.0, 6.0, ((1, 64),))
    norm_gain = jnp.clip(1.0 + 0.15 * jax.random.normal(keys[2], (SECTIONS, D), jnp.float32), 0.25, 1.75)
    expert_ids_keys = jax.random.split(jax.random.fold_in(keys[3], 1), SECTIONS * STEPS * TOKENS // TOK_DEV)
    expert_ids_turns = jax.random.permutation(jax.random.fold_in(keys[3], 3), SECTIONS * STEPS * TOKENS // TOK_DEV)
    expert_ids = jax.vmap(lambda own, number: assign_block(jax.random.fold_in(keys[3], 2), own, number, TOK_DEV, EXPERTS, TOP, CAP, 2))(expert_ids_keys, expert_ids_turns).reshape((SECTIONS, STEPS, TOKENS, TOP))
    gate_weights = jnp.clip(0.3 + 0.7 * jax.random.uniform(keys[4], (SECTIONS, STEPS, TOKENS, TOP), jnp.float32) ** shard_levels(keys[4], (SECTIONS, STEPS, TOKENS, TOP), ((0, 8), (2, 64)), -0.2, 0.2), 0.3, 1.0)
    w_gate = normal_values(keys[5], (SECTIONS, D, EXPERTS * FF), D ** -0.5, 0.125, ((0, 8), (2, 64)))
    w_up = normal_values(keys[6], (SECTIONS, D, EXPERTS * FF), D ** -0.5, 0.125, ((0, 8), (2, 64)))
    w_down = normal_values(keys[7], (SECTIONS, EXPERTS * FF, D), FF ** -0.5, 0.1875, ((0, 8), (1, 64)))
    return dict(carried=carried, incoming=incoming, norm_gain=norm_gain, expert_ids=expert_ids, gate_weights=gate_weights, w_gate=w_gate, w_up=w_up, w_down=w_down)


def moe_layer(token_block, norm_scale, route_ids, gate_vals, gate_mat, up_mat, down_mat):
    x_float = token_block.astype(jnp.float32)
    normed = (x_float * lax.rsqrt(lax.optimization_barrier(jnp.mean(x_float * x_float, axis=-1, keepdims=True)) + 1e-06) * norm_scale).astype(jnp.bfloat16)

    def add_expert(running, expert):
        offset = (expert * FF).astype(jnp.int32)
        gate_cols = lax.dynamic_slice_in_dim(gate_mat, offset, FF, 1)
        up_cols = lax.dynamic_slice_in_dim(up_mat, offset, FF, 1)
        down_rows = lax.dynamic_slice_in_dim(down_mat, offset, FF, 0)
        gate_act = jnp.dot(normed, gate_cols, preferred_element_type=jnp.float32)
        up_act = jnp.dot(normed, up_cols, preferred_element_type=jnp.float32)
        hidden = (jax.nn.silu(gate_act) * up_act).astype(jnp.bfloat16)
        partials = jnp.einsum('tsf,sfd->std', hidden.reshape(TOKENS, SPLIT, FF // SPLIT).astype(jnp.float32), down_rows.reshape(SPLIT, FF // SPLIT, D).astype(jnp.float32))
        partials = lax.optimization_barrier(partials.astype(jnp.bfloat16)).astype(jnp.float32)
        slot_weight = lax.optimization_barrier(jnp.sum(jnp.where(route_ids == expert, gate_vals, jnp.zeros_like(gate_vals)), axis=-1))
        return (running + slot_weight[:, None] * lax.optimization_barrier(jnp.sum(partials, axis=0)), None)
    running, _ = lax.scan(add_expert, jnp.zeros((TOKENS, D), jnp.float32), jnp.arange(EXPERTS, dtype=jnp.int32))
    return (x_float + running).astype(jnp.bfloat16)

def reference(carried, incoming, norm_gain, expert_ids, gate_weights, w_gate, w_up, w_down):
    states = [carried[section] for section in range(SECTIONS)]
    outputs = states
    for step_index in range(STEPS):
        outputs = [moe_layer(states[section], norm_gain[section], expert_ids[section, step_index], gate_weights[section, step_index], w_gate[section], w_up[section], w_down[section]) for section in range(SECTIONS)]
        if step_index + 1 < STEPS:
            states = [incoming[step_index]] + outputs[:-1]
    return jnp.stack(outputs, axis=0)
```

```python
import jax
import jax.numpy as jnp
from jax import lax
from jax.experimental import pallas as pl
from jax.experimental.pallas import tpu as pltpu
from jax.sharding import PartitionSpec as P

EXPERTS = 16
TOP = 2
STEPS = 2
CAP = 12
SPLIT = 4
RING = 8
PAIRS = RING // 2
MESH = pl.DeviceIdType.MESH


def routing(ids, gates):
    steps, tokens, _ = ids.shape
    flat = ids.reshape(steps, tokens * TOP)
    onehot = (flat[..., None] == jnp.arange(EXPERTS, dtype=jnp.int32)).astype(jnp.float32)
    below = jnp.tril(jnp.ones((tokens * TOP, tokens * TOP), jnp.float32), -1)
    before = jnp.einsum("ij,sje->sie", below, onehot, preferred_element_type=jnp.float32)
    position = jnp.sum(before * onehot, axis=-1)
    target = (flat.astype(jnp.float32) * CAP + position).reshape(steps, tokens, TOP)
    rows = jnp.concatenate([target, gates], axis=-1)
    rows = jnp.swapaxes(rows, 1, 2)
    rows = jnp.concatenate([rows, rows], axis=-1)
    return jnp.pad(rows, ((0, 0), (0, 4), (0, 0)))


def kernel(
    carried_ref, incoming_ref, gain_ref, meta_ref, wg_hbm, wu_hbm, wd_hbm,
    out_ref,
    state, tokens, meta, sent, rows, hidden, back, returned, part, parts, wg, wu, wd,
    w_sem, meta_ssem, meta_rsem, wd_ssem, wd_rsem,
    ring_ssem, ring_rsem, row_ssem, row_rsem, hid_ssem, hid_rsem,
    back_ssem, back_rsem, part_ssem, part_rsem, pass_ssem, pass_rsem,
):
    section = lax.axis_index("section")
    sections = lax.axis_size("section")
    me = lax.axis_index("expert")
    y, z = me // RING, me % RING
    half, q = z // SPLIT, z % SPLIT
    own = z // 2
    tok = carried_ref.shape[0]
    width = carried_ref.shape[1]
    slot = 2 * CAP
    cols = wd.shape[2]

    def at(yy, zz):
        return {"expert": yy * RING + zz}

    def remote(src, dst, ssem, rsem, device):
        return pltpu.make_async_remote_copy(
            src_ref=src, dst_ref=dst, send_sem=ssem, recv_sem=rsem, device_id=device, device_id_type=MESH
        )

    load_g = pltpu.make_async_copy(wg_hbm, wg, w_sem.at[0])
    load_u = pltpu.make_async_copy(wu_hbm, wu, w_sem.at[1])
    load_d = pltpu.make_async_copy(wd_hbm.at[:, pl.ds(pl.multiple_of(q * cols, cols), cols)], wd.at[q], w_sem.at[2])
    load_g.start()
    load_u.start()
    load_d.start()

    barrier = pltpu.get_barrier_semaphore()
    for d in range(1, RING):
        pl.semaphore_signal(barrier, inc=1, device_id=at(y, (z + d) % RING), device_id_type=MESH)
        pl.semaphore_signal(barrier, inc=1, device_id=at((y + d) % RING, z), device_id_type=MESH)

    @pl.when(section > 0)
    def _():
        pl.semaphore_signal(barrier, inc=1, device_id={"section": section - 1}, device_id_type=MESH)

    @pl.when(section < sections - 1)
    def _():
        pl.semaphore_signal(barrier, inc=1, device_id={"section": section + 1}, device_id_type=MESH)

    state[0] = carried_ref[...]
    linked = (section > 0).astype(jnp.int32) + (section < sections - 1).astype(jnp.int32)
    pl.semaphore_wait(barrier, 2 * (RING - 1) + linked)

    def meta_copy(d):
        return remote(meta_ref, meta.at[z], meta_ssem.at[d], meta_rsem.at[d], at(y, (z + d) % RING))

    meta_local = pltpu.make_async_copy(meta_ref, meta.at[z], meta_rsem.at[0])
    meta_local.start()
    for d in (1, 7, 2, 6, 3, 5, 4):
        meta_copy(d).start()

    def down_copy(d):
        other = (q + d) % SPLIT
        return remote(
            wd_hbm.at[:, pl.ds(pl.multiple_of(other * cols, cols), cols)], wd.at[q],
            wd_ssem.at[d], wd_rsem.at[d], at(y, half * SPLIT + other),
        )

    row_id = lax.broadcasted_iota(jnp.int32, (RING, slot, 2 * tok), 1)
    dest_id = lax.broadcasted_iota(jnp.int32, (RING, slot, 2 * tok), 0)
    lane_id = lax.broadcasted_iota(jnp.int32, (RING, slot, 2 * tok), 2)
    row_odd = (row_id >= CAP).astype(jnp.int32)
    lane_odd = (lane_id >= tok).astype(jnp.int32)
    key = dest_id * slot + half * CAP + row_id - CAP * row_odd
    key = jnp.where(row_odd == lane_odd, key, -1).astype(jnp.float32).reshape(RING * slot, 2 * tok)
    low_lane = lax.broadcasted_iota(jnp.int32, (1, 2 * tok), 1) < tok

    def step(st, carry):
        @pl.when(st == 1)
        def _():
            @pl.when(section == 0)
            def _():
                state[1] = incoming_ref[...]

            @pl.when(section > 0)
            def _():
                remote(out_ref, state.at[1], pass_ssem, pass_rsem, {"section": section}).wait_recv()

        x = state[st].astype(jnp.float32)
        scale = lax.rsqrt(jnp.mean(x * x, axis=-1, keepdims=True) + 1e-06)
        tokens[st, z] = (x * scale * gain_ref[...]).astype(jnp.bfloat16)

        def ring_copy(way, hop):
            sign = 1 - 2 * way
            origin = (z - sign * (hop - 1) + RING) % RING
            block = tokens.at[st, origin]
            if hop == RING // 2:
                block = block.at[pl.ds(way * (tok // 2), tok // 2)]
            return remote(
                block, block, ring_ssem.at[way, hop - 1], ring_rsem.at[st, way, hop - 1], at(y, (z + sign + RING) % RING)
            )

        def hop(n):
            for way in range(2):
                ring_copy(way, n).wait_recv()
                if n < RING // 2:
                    ring_copy(way, n + 1).start()

        def lanes(pair, row):
            return jnp.where(low_lane, meta[2 * pair, st, row : row + 1, :], meta[2 * pair + 1, st, row : row + 1, :])

        def row_copy(pair, d):
            dest = (y + d) % RING
            return remote(
                sent.at[pair, dest], rows.at[st, pair, y], row_ssem.at[pair, d], row_rsem.at[st, pair, d], at(dest, z)
            )

        def row_local(pair):
            return pltpu.make_async_copy(sent.at[pair, y], rows.at[st, pair, y], row_rsem.at[st, pair, 0])

        def select(pair):
            pick = ((key == lanes(pair, 0)) | (key == lanes(pair, 1))).astype(jnp.bfloat16)
            block = tokens[st, pl.ds(2 * pair, 2)].reshape(2 * tok, width)
            for c in range(0, width, 512):
                got = jnp.dot(pick, block[:, c : c + 512], preferred_element_type=jnp.float32)
                sent[pair, :, :, c : c + 512] = got.astype(jnp.bfloat16).reshape(RING, slot, 512)
            for d in (4, 3, 5, 2, 6, 1, 7):
                row_copy(pair, d).start()
            row_local(pair).start()

        def hidden_copy(pair, d):
            return remote(
                hidden.at[st, pair, q], hidden.at[st, pair, q], hid_ssem.at[pair, d], hid_rsem.at[st, pair, d],
                at(y, half * SPLIT + (q + d) % SPLIT),
            )

        def forward(pair):
            row_local(pair).wait()
            for d in range(1, RING):
                row_copy(pair, d).wait_recv()
            arrived = rows[st, pair].reshape(RING * slot, width)
            gate = jnp.dot(arrived, wg[...], preferred_element_type=jnp.float32)
            up = jnp.dot(arrived, wu[...], preferred_element_type=jnp.float32)
            act = gate / (1.0 + jnp.exp(-gate)) * up
            hidden[st, pair, q] = act.astype(jnp.bfloat16)
            for d in (1, 3, 2):
                hidden_copy(pair, d).start()

        def back_copy(pair, d):
            dest = (y + d) % RING
            return remote(
                back.at[pair, dest], returned.at[st, pair, y], back_ssem.at[pair, d], back_rsem.at[st, pair, d], at(dest, z)
            )

        def back_local(pair):
            return pltpu.make_async_copy(back.at[pair, y], returned.at[st, pair, y], back_rsem.at[st, pair, 0])

        def down(pair):
            for d in range(1, SPLIT):
                hidden_copy(pair, d).wait_recv()
            total = jnp.dot(hidden[st, pair, 0], wd[0], preferred_element_type=jnp.float32)
            for k in range(1, SPLIT):
                total += jnp.dot(hidden[st, pair, k], wd[k], preferred_element_type=jnp.float32)
            back[pair] = total.astype(jnp.bfloat16).reshape(RING, slot, cols)
            for d in (4, 3, 5, 2, 6, 1, 7):
                back_copy(pair, d).start()
            back_local(pair).start()

        def part_copy(pair, b):
            dest = 2 * pair + b
            return remote(
                part.at[pair, b], parts.at[st, z], part_ssem.at[pair, b], part_rsem.at[st, (dest - z + RING) % RING], at(y, dest)
            )

        def part_local(pair, b):
            return pltpu.make_async_copy(part.at[pair, b], parts.at[st, z], part_rsem.at[st, 0])

        def combine(pair):
            back_local(pair).wait()
            for d in range(1, RING):
                back_copy(pair, d).wait_recv()
            mix = jnp.where(key == lanes(pair, 0), lanes(pair, 2), 0.0) + jnp.where(key == lanes(pair, 1), lanes(pair, 3), 0.0)
            high = mix.astype(jnp.bfloat16)
            low = (mix - high.astype(jnp.float32)).astype(jnp.bfloat16)
            values = returned[st, pair].reshape(RING * slot, cols)
            dims = (((0,), (0,)), ((), ()))
            total = lax.dot_general(high, values, dims, preferred_element_type=jnp.float32)
            total += lax.dot_general(low, values, dims, preferred_element_type=jnp.float32)
            part[pair] = total.astype(jnp.bfloat16).reshape(2, tok, cols)
            for b in range(2):
                @pl.when(2 * pair + b == z)
                def _():
                    part_local(pair, b).start()

                @pl.when(2 * pair + b != z)
                def _():
                    part_copy(pair, b).start()

        mine, sibling = own, half * 2 + (1 - own % 2)
        first, second = half * 2, half * 2 + 1
        third, fourth = (half * 2 + 2) % PAIRS, (half * 2 + 3) % PAIRS

        for way in range(2):
            ring_copy(way, 1).start()

        @pl.when(st == 0)
        def _():
            for d in range(1, SPLIT):
                down_copy(d).start()
            meta_local.wait()
            for d in range(1, RING):
                meta_copy(d).wait_recv()

        hop(1)
        select(mine)
        hop(2)
        hop(3)
        select(sibling)
        hop(4)
        select(third)
        select(fourth)

        @pl.when(st == 0)
        def _():
            load_g.wait()
            load_u.wait()

        forward(mine)
        forward(sibling)

        @pl.when(st == 0)
        def _():
            load_d.wait()
            for d in range(1, SPLIT):
                down_copy(d).wait_recv()

        down(first)
        down(second)
        combine(first)
        combine(second)
        forward(third)
        down(third)
        combine(third)
        forward(fourth)
        down(fourth)
        combine(fourth)

        part_own = pltpu.make_async_copy(part.at[0, 0], parts.at[st, z], part_rsem.at[st, 0])
        part_own.wait()
        for d in range(1, RING):
            remote(part.at[0, 0], parts.at[st, z], part_ssem.at[0, 0], part_rsem.at[st, d], at(y, z)).wait_recv()
        for k in range(SPLIT):
            span = slice(k * cols, (k + 1) * cols)
            total = parts[st, k].astype(jnp.float32) + parts[st, SPLIT + k].astype(jnp.float32)
            out_ref[:, span] = (state[st, :, span].astype(jnp.float32) + total).astype(jnp.bfloat16)

        pass_on = remote(out_ref, state.at[1], pass_ssem, pass_rsem, {"section": section + 1})

        @pl.when((st == 0) & (section < sections - 1))
        def _():
            pass_on.start()

        for way in range(2):
            for n in range(1, RING // 2 + 1):
                ring_copy(way, n).wait_send()
        for pair in range(PAIRS):
            for d in range(1, RING):
                row_copy(pair, d).wait_send()
                back_copy(pair, d).wait_send()
            for d in range(1, SPLIT):
                hidden_copy(pair, d).wait_send()
            for b in range(2):
                @pl.when(2 * pair + b != z)
                def _():
                    part_copy(pair, b).wait_send()

        @pl.when((st == 0) & (section < sections - 1))
        def _():
            pass_on.wait_send()

        return carry

    lax.fori_loop(0, STEPS, step, 0)
    for d in range(1, RING):
        meta_copy(d).wait_send()
    for d in range(1, SPLIT):
        down_copy(d).wait_send()


def on_device(carried, incoming, norm_gain, expert_ids, gate_weights, w_gate, w_up, w_down):
    meta = routing(expert_ids[0], gate_weights[0])
    tok, width = carried.shape[1:]
    units = w_gate.shape[2]
    cols = width // SPLIT
    slot = 2 * CAP
    lanes = meta.shape[-1]
    bf16 = jnp.bfloat16
    dma = pltpu.SemaphoreType.DMA
    vmem = pl.BlockSpec(memory_space=pltpu.VMEM)
    hbm = pl.BlockSpec(memory_space=pl.ANY)
    out = pl.pallas_call(
        kernel,
        out_shape=jax.ShapeDtypeStruct((tok, width), bf16),
        in_specs=[vmem] * 4 + [hbm] * 3,
        out_specs=vmem,
        scratch_shapes=[
            pltpu.VMEM((STEPS, tok, width), bf16),
            pltpu.VMEM((STEPS, RING, tok, width), bf16),
            pltpu.VMEM((RING, STEPS, 8, lanes), jnp.float32),
            pltpu.VMEM((PAIRS, RING, slot, width), bf16),
            pltpu.VMEM((STEPS, PAIRS, RING, slot, width), bf16),
            pltpu.VMEM((STEPS, PAIRS, SPLIT, RING * slot, units), bf16),
            pltpu.VMEM((PAIRS, RING, slot, cols), bf16),
            pltpu.VMEM((STEPS, PAIRS, RING, slot, cols), bf16),
            pltpu.VMEM((PAIRS, 2, tok, cols), bf16),
            pltpu.VMEM((STEPS, RING, tok, cols), bf16),
            pltpu.VMEM((width, units), bf16),
            pltpu.VMEM((width, units), bf16),
            pltpu.VMEM((SPLIT, units, cols), bf16),
            dma((3,)), dma((RING,)), dma((RING,)), dma((SPLIT,)), dma((SPLIT,)),
            dma((2, 4)), dma((STEPS, 2, 4)),
            dma((PAIRS, RING)), dma((STEPS, PAIRS, RING)),
            dma((PAIRS, SPLIT)), dma((STEPS, PAIRS, SPLIT)),
            dma((PAIRS, RING)), dma((STEPS, PAIRS, RING)),
            dma((PAIRS, 2)), dma((STEPS, RING)),
            dma, dma,
        ],
        compiler_params=pltpu.CompilerParams(
            collective_id=0, has_side_effects=True, vmem_limit_bytes=48 * 1024 * 1024
        ),
    )(carried[0], incoming[0], norm_gain, meta, w_gate[0], w_up[0], w_down[0])
    return out[None]


def solution(mesh):
    return jax.shard_map(
        on_device,
        mesh=mesh,
        in_specs=(
            P("section", "expert", None),
            P(None, "expert", None),
            P("section", None),
            P("section", None, "expert", None),
            P("section", None, "expert", None),
            P("section", None, "expert"),
            P("section", None, "expert"),
            P("section", "expert", None),
        ),
        out_specs=P("section", "expert", None),
        check_vma=False,
    )
```

```python
import jax
import jax.numpy as jnp
from jax import lax
from jax.experimental import pallas as pl
from jax.experimental.pallas import tpu as pltpu
from jax.sharding import PartitionSpec as P

EXPERTS = 16
TOP = 2
STEPS = 2
CAP = 12
SPLIT = 4
RING = 8
PAIRS = RING // 2
MESH = pl.DeviceIdType.MESH
NEAR_ONE = True
FAR_FIRST = (4, 3, 5, 2, 6, 1, 7)


def routing(st, ids_ref, gates_ref, meta_ref):
    twice = lambda row: jnp.concatenate([row, row], axis=1)
    tok = ids_ref.shape[2]
    first, second = twice(ids_ref[st, 0:1, :]), twice(ids_ref[st, 1:2, :])
    expert = lax.broadcasted_iota(jnp.int32, (EXPERTS, 2 * tok), 0)
    lane = lax.broadcasted_iota(jnp.int32, (2 * tok, 2 * tok), 1)
    ahead = lax.broadcasted_iota(jnp.int32, (2 * tok, 2 * tok), 0) < lane - jnp.where(lane >= tok, tok, 0)
    ahead = ahead.astype(jnp.bfloat16)
    in_first = (expert == first).astype(jnp.float32)
    in_second = (expert == second).astype(jnp.float32)
    count = lambda hot: jnp.dot(hot.astype(jnp.bfloat16), ahead, preferred_element_type=jnp.float32)
    total = 0.5 * jnp.sum(in_first, axis=1, keepdims=True)
    place_first = jnp.sum(in_first * count(in_first), axis=0, keepdims=True)
    place_second = jnp.sum(in_second * (count(in_second) + total), axis=0, keepdims=True)
    meta_ref[st, 0:1, :] = first.astype(jnp.float32) * CAP + place_first
    meta_ref[st, 1:2, :] = second.astype(jnp.float32) * CAP + place_second
    meta_ref[st, 2:3, :] = twice(gates_ref[st, 0:1, :])
    meta_ref[st, 3:4, :] = twice(gates_ref[st, 1:2, :])
    meta_ref[st, 4:8, :] = jnp.zeros((4, 2 * tok), jnp.float32)


def kernel(
    carried_ref, incoming_ref, gain_ref, ids_ref, gates_ref, wg_hbm, wu_hbm, wd_hbm,
    out_ref,
    state, tokens, meta_ref, meta, sent, rows, sent_one, rows_one, hidden, back, returned, part, parts, wg, wu, wd,
    w_sem, meta_ssem, meta_rsem, wd_ssem, wd_rsem,
    ring_ssem, ring_rsem, row_ssem, row_rsem, one_ssem, one_rsem, relay_ssem, relay_rsem, hid_ssem, hid_rsem,
    back_ssem, back_rsem, part_ssem, part_rsem, pass_ssem, pass_rsem,
):
    section = lax.axis_index("section")
    sections = lax.axis_size("section")
    me = lax.axis_index("expert")
    y, z = me // RING, me % RING
    half, q = z // SPLIT, z % SPLIT
    own = z // 2
    par = z % 2
    mate = z + 1 - 2 * par
    peer = q + 1 - 2 * par
    inner = 1 + q // 2
    other = 2 - q // 2
    other_outer = 3 - 3 * (q // 2)
    tok = carried_ref.shape[0]
    width = carried_ref.shape[1]
    slot = 2 * CAP
    cols = wd.shape[2]
    span = width // 2

    def at(yy, zz):
        return {"expert": yy * RING + zz}

    def remote(src, dst, ssem, rsem, device):
        return pltpu.make_async_remote_copy(
            src_ref=src, dst_ref=dst, send_sem=ssem, recv_sem=rsem, device_id=device, device_id_type=MESH
        )

    load_g = pltpu.make_async_copy(wg_hbm, wg, w_sem.at[0])
    load_u = pltpu.make_async_copy(wu_hbm, wu, w_sem.at[1])
    load_d = pltpu.make_async_copy(wd_hbm.at[:, pl.ds(pl.multiple_of(q * cols, cols), cols)], wd.at[q], w_sem.at[2])
    load_g.start()
    load_u.start()
    load_d.start()

    barrier = pltpu.get_barrier_semaphore()
    for d in range(1, RING):
        pl.semaphore_signal(barrier, inc=1, device_id=at(y, (z + d) % RING), device_id_type=MESH)
        pl.semaphore_signal(barrier, inc=1, device_id=at((y + d) % RING, z), device_id_type=MESH)

    @pl.when(section > 0)
    def _():
        pl.semaphore_signal(barrier, inc=1, device_id={"section": section - 1}, device_id_type=MESH)

    @pl.when(section < sections - 1)
    def _():
        pl.semaphore_signal(barrier, inc=1, device_id={"section": section + 1}, device_id_type=MESH)

    state[0] = carried_ref[...]
    for st in range(STEPS):
        routing(st, ids_ref, gates_ref, meta_ref)
    linked = (section > 0).astype(jnp.int32) + (section < sections - 1).astype(jnp.int32)
    pl.semaphore_wait(barrier, 2 * (RING - 1) + linked)

    def meta_copy(d):
        return remote(meta_ref, meta.at[z], meta_ssem.at[d], meta_rsem.at[d], at(y, (z + d) % RING))

    meta_local = pltpu.make_async_copy(meta_ref, meta.at[z], meta_rsem.at[0])
    meta_local.start()
    for d in (1, 7, 2, 6, 3, 5, 4):
        meta_copy(d).start()

    def down_copy(d):
        other = (q + d) % SPLIT
        return remote(
            wd_hbm.at[:, pl.ds(pl.multiple_of(other * cols, cols), cols)], wd.at[q],
            wd_ssem.at[d], wd_rsem.at[d], at(y, half * SPLIT + other),
        )

    row_id = lax.broadcasted_iota(jnp.int32, (RING, slot, 2 * tok), 1)
    dest_id = lax.broadcasted_iota(jnp.int32, (RING, slot, 2 * tok), 0)
    lane_id = lax.broadcasted_iota(jnp.int32, (RING, slot, 2 * tok), 2)
    row_odd = (row_id >= CAP).astype(jnp.int32)
    lane_odd = (lane_id >= tok).astype(jnp.int32)
    key = dest_id * slot + half * CAP + row_id - CAP * row_odd
    key = jnp.where(row_odd == lane_odd, key, -1).astype(jnp.float32).reshape(RING * slot, 2 * tok)
    odd_row = lax.broadcasted_iota(jnp.int32, (RING, slot, wg.shape[1]), 1).reshape(RING * slot, wg.shape[1]) >= CAP
    low_lane = lax.broadcasted_iota(jnp.int32, (1, 2 * tok), 1) < tok

    def step(st, carry):
        @pl.when(st == 1)
        def _():
            @pl.when(section == 0)
            def _():
                state[1] = incoming_ref[...]

            @pl.when(section > 0)
            def _():
                remote(out_ref, state.at[1], pass_ssem, pass_rsem, {"section": section}).wait_recv()

        x = state[st].astype(jnp.float32)
        scale = lax.rsqrt(jnp.mean(x * x, axis=-1, keepdims=True) + 1e-06)
        tokens[st, z] = (x * scale * gain_ref[...]).astype(jnp.bfloat16)

        def ring_copy(way, hop):
            sign = 1 - 2 * way
            origin = (z - sign * (hop - 1) + RING) % RING
            block = tokens.at[st, origin]
            if hop == RING // 2:
                block = block.at[pl.ds(way * (tok // 2), tok // 2)]
            return remote(
                block, block, ring_ssem.at[way, hop - 1], ring_rsem.at[st, way, hop - 1], at(y, (z + sign + RING) % RING)
            )

        def hop(n):
            for way in range(2):
                ring_copy(way, n).wait_recv()
                if n < RING // 2:
                    ring_copy(way, n + 1).start()

        def lanes(pair, row):
            return jnp.where(low_lane, meta[2 * pair, st, row : row + 1, :], meta[2 * pair + 1, st, row : row + 1, :])

        def row_copy(n, d):
            dest = (y + d) % RING
            return remote(sent.at[n, dest], rows.at[st, n, y], row_ssem.at[n, d], row_rsem.at[st, n, d], at(dest, z))

        def row_local(n):
            return pltpu.make_async_copy(sent.at[n, y], rows.at[st, n, y], row_rsem.at[st, n, 0])

        def select(n, pair):
            pick = ((key == lanes(pair, 0)) | (key == lanes(pair, 1))).astype(jnp.bfloat16)
            block = tokens[st, pl.ds(2 * pair, 2)].reshape(2 * tok, width)
            for c in range(0, width, 512):
                got = jnp.dot(pick, block[:, c : c + 512], preferred_element_type=jnp.float32)
                sent[n, :, :, c : c + 512] = got.astype(jnp.bfloat16).reshape(RING, slot, 512)
            for d in FAR_FIRST:
                row_copy(n, d).start()
            row_local(n).start()

        def one_place(i):
            return rows_one.at[st, (0, 0, 1, 2)[i], 1 - par if i == 1 else par]

        def one_copy(i, d):
            dest = (y + d) % RING
            return remote(
                sent_one.at[i, dest], one_place(i).at[y], one_ssem.at[i, d], one_rsem.at[st, i, d], at(dest, z)
            )

        def one_local(i):
            return pltpu.make_async_copy(sent_one.at[i, y], one_place(i).at[y], one_rsem.at[st, i, 0])

        def select_one(i, column):
            pick = (key == meta[column, st, 0:1, :]) | (key == meta[column, st, 1:2, :])
            block = jnp.concatenate([tokens[st, column, :, :span], tokens[st, column, :, span:]], axis=0)
            for c in range(0, span, 512):
                got = jnp.dot(pick.astype(jnp.bfloat16), block[:, c : c + 512], preferred_element_type=jnp.float32)
                sent_one[i, :, :, c : c + 512] = got.astype(jnp.bfloat16).reshape(RING, slot, 512)
            for d in FAR_FIRST:
                one_copy(i, d).start()
            one_local(i).start()

        def one_wait(i, d):
            if d == 0:
                one_local(i).wait()
            else:
                one_copy(i, d).wait_recv()

        def relay_copy(c, d, mine):
            place = rows_one.at[st, c, par if mine else 1 - par, (y - d + RING) % RING]
            return remote(place, place, relay_ssem.at[c - 1, d], relay_rsem.at[st, c - 1, d], at(y, mate))

        def relay(c):
            for d in (0, 1, 7, 2, 6, 3, 5, 4):
                one_wait(c + 1, d)
                relay_copy(c, d, True).start()

        def hidden_copy(pair, source, k, device):
            block = hidden.at[st, pair, source]
            return remote(block, block, hid_ssem.at[pair, k], hid_rsem.at[st, pair, source], at(y, half * SPLIT + device))

        def hidden_pass(pair):
            @pl.when(inner == q)
            def _():
                for k, source in enumerate((other, other_outer)):
                    hidden_copy(pair, source, 2 + k, q).wait_recv()
                    hidden_copy(pair, source, 2 + k, peer).start()

        def share(pair, gate, up):
            act = gate / (1.0 + jnp.exp(-gate)) * up
            hidden[st, pair, q] = act.astype(jnp.bfloat16)
            hidden_copy(pair, q, 0, other).start()
            hidden_copy(pair, q, 1, peer).start()

        def forward(n, pair):
            row_local(n).wait()
            for d in range(1, RING):
                row_copy(n, d).wait_recv()
            arrived = rows[st, n].reshape(RING * slot, width)
            gate = jnp.dot(arrived, wg[...], preferred_element_type=jnp.float32)
            up = jnp.dot(arrived, wu[...], preferred_element_type=jnp.float32)
            share(pair, gate, up)

        def forward_one(c, pair):
            for d in range(RING):
                if c == 0:
                    one_wait(0, d)
                    one_wait(1, d)
                else:
                    relay_copy(c, d, False).wait_recv()
            even = rows_one[st, c, 0].reshape(RING * slot, span)
            odd = rows_one[st, c, 1].reshape(RING * slot, span)

            def project(w):
                top, bottom = w[:span], w[span:]
                dot = lambda a, b: jnp.dot(a, b, preferred_element_type=jnp.float32)
                from_even = dot(even, top) + pltpu.roll(dot(even, bottom), RING * slot - CAP, 0)
                from_odd = pltpu.roll(dot(odd, top), CAP, 0) + dot(odd, bottom)
                return jnp.where(odd_row, from_odd, from_even)

            share(pair, project(wg), project(wu))

        def back_copy(pair, d):
            dest = (y + d) % RING
            return remote(
                back.at[pair, dest], returned.at[st, pair, y], back_ssem.at[pair, d], back_rsem.at[st, pair, d], at(dest, z)
            )

        def back_local(pair):
            return pltpu.make_async_copy(back.at[pair, y], returned.at[st, pair, y], back_rsem.at[st, pair, 0])

        def down(pair):
            hidden_copy(pair, peer, 0, q).wait_recv()

            @pl.when(inner != q)
            def _():
                for source in (other, other_outer):
                    hidden_copy(pair, source, 0, q).wait_recv()

            total = jnp.dot(hidden[st, pair, 0], wd[0], preferred_element_type=jnp.float32)
            for k in range(1, SPLIT):
                total += jnp.dot(hidden[st, pair, k], wd[k], preferred_element_type=jnp.float32)
            back[pair] = total.astype(jnp.bfloat16).reshape(RING, slot, cols)
            for d in (4, 3, 5, 2, 6, 1, 7):
                back_copy(pair, d).start()
            back_local(pair).start()

        def part_copy(pair, b):
            dest = 2 * pair + b
            return remote(
                part.at[pair, b], parts.at[st, z], part_ssem.at[pair, b], part_rsem.at[st, (dest - z + RING) % RING], at(y, dest)
            )

        def part_local(pair, b):
            return pltpu.make_async_copy(part.at[pair, b], parts.at[st, z], part_rsem.at[st, 0])

        def combine(pair):
            back_local(pair).wait()
            for d in range(1, RING):
                back_copy(pair, d).wait_recv()
            mix = jnp.where(key == lanes(pair, 0), lanes(pair, 2), 0.0) + jnp.where(key == lanes(pair, 1), lanes(pair, 3), 0.0)
            high = mix.astype(jnp.bfloat16)
            low = (mix - high.astype(jnp.float32)).astype(jnp.bfloat16)
            values = returned[st, pair].reshape(RING * slot, cols)
            dims = (((0,), (0,)), ((), ()))
            total = lax.dot_general(high, values, dims, preferred_element_type=jnp.float32)
            total += lax.dot_general(low, values, dims, preferred_element_type=jnp.float32)
            part[pair] = total.astype(jnp.bfloat16).reshape(2, tok, cols)
            for b in range(2):
                @pl.when(2 * pair + b == z)
                def _():
                    part_local(pair, b).start()

                @pl.when(2 * pair + b != z)
                def _():
                    part_copy(pair, b).start()

        sibling, near, far = own + 1 - 2 * (own % 2), PAIRS - 1 - own, (own + 2) % PAIRS
        first, second = half * 2, half * 2 + 1
        third, fourth = (half * 2 + 2) % PAIRS, (half * 2 + 3) % PAIRS

        for way in range(2):
            ring_copy(way, 1).start()

        @pl.when(st == 0)
        def _():
            meta_local.wait()

        select_one(0, z)

        @pl.when(st == 0)
        def _():
            for d in (1, 7):
                meta_copy(d).wait_recv()

        hop(1)
        select_one(1, mate)

        @pl.when(st == 0)
        def _():
            for d in range(2, 7):
                meta_copy(d).wait_recv()

        hop(2)
        select_one(2, 2 * sibling + par)
        if NEAR_ONE:
            select_one(3, 2 * near + par)

        @pl.when(st == 0)
        def _():
            load_g.wait()
            load_u.wait()

        forward_one(0, own)
        hop(3)

        @pl.when(st == 0)
        def _():
            for d in range(1, SPLIT):
                down_copy(d).start()

        if not NEAR_ONE:
            select(0, near)
        relay(1)
        hop(4)
        select(1, far)

        if NEAR_ONE:
            relay(2)
        forward_one(1, sibling)
        hidden_pass(first)
        hidden_pass(second)
        if NEAR_ONE:
            forward_one(2, near)
        else:
            forward(0, near)

        @pl.when(st == 0)
        def _():
            load_d.wait()
            for d in range(1, SPLIT):
                down_copy(d).wait_recv()

        down(first)
        down(second)
        forward(1, far)
        combine(first)
        combine(second)
        hidden_pass(third)
        hidden_pass(fourth)
        down(third)
        down(fourth)
        combine(third)
        combine(fourth)

        part_own = pltpu.make_async_copy(part.at[0, 0], parts.at[st, z], part_rsem.at[st, 0])
        part_own.wait()
        for d in range(1, RING):
            remote(part.at[0, 0], parts.at[st, z], part_ssem.at[0, 0], part_rsem.at[st, d], at(y, z)).wait_recv()
        for k in range(SPLIT):
            block = slice(k * cols, (k + 1) * cols)
            total = parts[st, k].astype(jnp.float32) + parts[st, SPLIT + k].astype(jnp.float32)
            out_ref[:, block] = (state[st, :, block].astype(jnp.float32) + total).astype(jnp.bfloat16)

        pass_on = remote(out_ref, state.at[1], pass_ssem, pass_rsem, {"section": section + 1})

        @pl.when((st == 0) & (section < sections - 1))
        def _():
            pass_on.start()

        for way in range(2):
            for n in range(1, RING // 2 + 1):
                ring_copy(way, n).wait_send()
        for d in range(1, RING):
            for n in range(1 if NEAR_ONE else 0, 2):
                row_copy(n, d).wait_send()
            for i in range(4 if NEAR_ONE else 3):
                one_copy(i, d).wait_send()
        for c in range(1, 3 if NEAR_ONE else 2):
            for d in range(RING):
                relay_copy(c, d, True).wait_send()
        for pair in range(PAIRS):
            for d in range(1, RING):
                back_copy(pair, d).wait_send()
            hidden_copy(pair, q, 0, other).wait_send()
            hidden_copy(pair, q, 1, peer).wait_send()

            @pl.when(inner == q)
            def _():
                for k, source in enumerate((other, other_outer)):
                    hidden_copy(pair, source, 2 + k, peer).wait_send()

            for b in range(2):
                @pl.when(2 * pair + b != z)
                def _():
                    part_copy(pair, b).wait_send()

        @pl.when((st == 0) & (section < sections - 1))
        def _():
            pass_on.wait_send()

        return carry

    lax.fori_loop(0, STEPS, step, 0)
    for d in range(1, RING):
        meta_copy(d).wait_send()
    for d in range(1, SPLIT):
        down_copy(d).wait_send()


def on_device(carried, incoming, norm_gain, expert_ids, gate_weights, w_gate, w_up, w_down):
    ids, gates = jnp.swapaxes(expert_ids[0], 1, 2), jnp.swapaxes(gate_weights[0], 1, 2)
    tok, width = carried.shape[1:]
    units = w_gate.shape[2]
    cols = width // SPLIT
    slot = 2 * CAP
    lanes = 2 * tok
    bf16 = jnp.bfloat16
    dma = pltpu.SemaphoreType.DMA
    vmem = pl.BlockSpec(memory_space=pltpu.VMEM)
    hbm = pl.BlockSpec(memory_space=pl.ANY)
    out = pl.pallas_call(
        kernel,
        out_shape=jax.ShapeDtypeStruct((tok, width), bf16),
        in_specs=[vmem] * 5 + [hbm] * 3,
        out_specs=vmem,
        scratch_shapes=[
            pltpu.VMEM((STEPS, tok, width), bf16),
            pltpu.VMEM((STEPS, RING, tok, width), bf16),
            pltpu.VMEM((STEPS, 8, lanes), jnp.float32),
            pltpu.VMEM((RING, STEPS, 8, lanes), jnp.float32),
            pltpu.VMEM((2, RING, slot, width), bf16),
            pltpu.VMEM((STEPS, 2, RING, slot, width), bf16),
            pltpu.VMEM((4, RING, slot, width // 2), bf16),
            pltpu.VMEM((STEPS, 3, 2, RING, slot, width // 2), bf16),
            pltpu.VMEM((STEPS, PAIRS, SPLIT, RING * slot, units), bf16),
            pltpu.VMEM((PAIRS, RING, slot, cols), bf16),
            pltpu.VMEM((STEPS, PAIRS, RING, slot, cols), bf16),
            pltpu.VMEM((PAIRS, 2, tok, cols), bf16),
            pltpu.VMEM((STEPS, RING, tok, cols), bf16),
            pltpu.VMEM((width, units), bf16),
            pltpu.VMEM((width, units), bf16),
            pltpu.VMEM((SPLIT, units, cols), bf16),
            dma((3,)), dma((RING,)), dma((RING,)), dma((SPLIT,)), dma((SPLIT,)),
            dma((2, 4)), dma((STEPS, 2, 4)),
            dma((2, RING)), dma((STEPS, 2, RING)),
            dma((4, RING)), dma((STEPS, 4, RING)),
            dma((2, RING)), dma((STEPS, 2, RING)),
            dma((PAIRS, SPLIT)), dma((STEPS, PAIRS, SPLIT)),
            dma((PAIRS, RING)), dma((STEPS, PAIRS, RING)),
            dma((PAIRS, 2)), dma((STEPS, RING)),
            dma, dma,
        ],
        compiler_params=pltpu.CompilerParams(
            collective_id=0, has_side_effects=True, vmem_limit_bytes=62 * 1024 * 1024
        ),
    )(carried[0], incoming[0], norm_gain, ids, gates, w_gate[0], w_up[0], w_down[0])
    return out[None]


def solution(mesh):
    return jax.shard_map(
        on_device,
        mesh=mesh,
        in_specs=(
            P("section", "expert", None),
            P(None, "expert", None),
            P("section", None),
            P("section", None, "expert", None),
            P("section", None, "expert", None),
            P("section", None, "expert"),
            P("section", None, "expert"),
            P("section", "expert", None),
        ),
        out_specs=P("section", "expert", None),
        check_vma=False,
    )
```

```python
import jax
import jax.numpy as jnp
from jax import lax
from jax.experimental import pallas as pl
from jax.experimental.pallas import tpu as pltpu
from jax.sharding import PartitionSpec as P

EXPERTS = 16
TOP = 2
STEPS = 2
CAP = 12
SPLIT = 4
RING = 8
PAIRS = RING // 2
MESH = pl.DeviceIdType.MESH
NEAR_ONE = True
FAR_FIRST = (4, 3, 5, 2, 6, 1, 7)


def routing(st, ids_ref, gates_ref, meta_ref):
    twice = lambda row: jnp.concatenate([row, row], axis=1)
    tok = ids_ref.shape[2]
    first, second = twice(ids_ref[st, 0:1, :]), twice(ids_ref[st, 1:2, :])
    expert = lax.broadcasted_iota(jnp.int32, (EXPERTS, 2 * tok), 0)
    lane = lax.broadcasted_iota(jnp.int32, (2 * tok, 2 * tok), 1)
    ahead = lax.broadcasted_iota(jnp.int32, (2 * tok, 2 * tok), 0) < lane - jnp.where(lane >= tok, tok, 0)
    ahead = ahead.astype(jnp.bfloat16)
    in_first = (expert == first).astype(jnp.float32)
    in_second = (expert == second).astype(jnp.float32)
    count = lambda hot: jnp.dot(hot.astype(jnp.bfloat16), ahead, preferred_element_type=jnp.float32)
    total = 0.5 * jnp.sum(in_first, axis=1, keepdims=True)
    place_first = jnp.sum(in_first * count(in_first), axis=0, keepdims=True)
    place_second = jnp.sum(in_second * (count(in_second) + total), axis=0, keepdims=True)
    meta_ref[st, 0:1, :] = first.astype(jnp.float32) * CAP + place_first
    meta_ref[st, 1:2, :] = second.astype(jnp.float32) * CAP + place_second
    meta_ref[st, 2:3, :] = twice(gates_ref[st, 0:1, :])
    meta_ref[st, 3:4, :] = twice(gates_ref[st, 1:2, :])
    meta_ref[st, 4:8, :] = jnp.zeros((4, 2 * tok), jnp.float32)


def kernel(
    carried_ref, incoming_ref, gain_ref, ids_ref, gates_ref, wg_hbm, wu_hbm, wd_hbm,
    out_ref,
    state, tokens, meta_ref, meta, sent, rows, sent_one, rows_one, hidden, back, returned, part, parts, wg, wu, wd,
    w_sem, meta_ssem, meta_rsem, wd_ssem, wd_rsem,
    ring_ssem, ring_rsem, row_ssem, row_rsem, one_ssem, one_rsem, relay_ssem, relay_rsem, hid_ssem, hid_rsem,
    back_ssem, back_rsem, part_ssem, part_rsem, pass_ssem, pass_rsem,
):
    section = lax.axis_index("section")
    sections = lax.axis_size("section")
    me = lax.axis_index("expert")
    y, z = me // RING, me % RING
    half, q = z // SPLIT, z % SPLIT
    own = z // 2
    par = z % 2
    mate = z + 1 - 2 * par
    peer = q + 1 - 2 * par
    other = 2 - q // 2
    other_outer = 3 - 3 * (q // 2)
    tok = carried_ref.shape[0]
    width = carried_ref.shape[1]
    slot = 2 * CAP
    cols = wd.shape[2]
    span = width // 2

    def at(yy, zz):
        return {"expert": yy * RING + zz}

    def remote(src, dst, ssem, rsem, device):
        return pltpu.make_async_remote_copy(
            src_ref=src, dst_ref=dst, send_sem=ssem, recv_sem=rsem, device_id=device, device_id_type=MESH
        )

    load_g = pltpu.make_async_copy(wg_hbm, wg, w_sem.at[0])
    load_u = pltpu.make_async_copy(wu_hbm, wu, w_sem.at[1])
    load_d = pltpu.make_async_copy(wd_hbm.at[:, pl.ds(pl.multiple_of(q * cols, cols), cols)], wd.at[q], w_sem.at[2])
    load_g.start()
    load_u.start()
    load_d.start()

    barrier = pltpu.get_barrier_semaphore()
    for d in range(1, RING):
        pl.semaphore_signal(barrier, inc=1, device_id=at(y, (z + d) % RING), device_id_type=MESH)
        pl.semaphore_signal(barrier, inc=1, device_id=at((y + d) % RING, z), device_id_type=MESH)

    @pl.when(section > 0)
    def _():
        pl.semaphore_signal(barrier, inc=1, device_id={"section": section - 1}, device_id_type=MESH)

    @pl.when(section < sections - 1)
    def _():
        pl.semaphore_signal(barrier, inc=1, device_id={"section": section + 1}, device_id_type=MESH)

    state[0] = carried_ref[...]
    for st in range(STEPS):
        routing(st, ids_ref, gates_ref, meta_ref)
    linked = (section > 0).astype(jnp.int32) + (section < sections - 1).astype(jnp.int32)
    pl.semaphore_wait(barrier, 2 * (RING - 1) + linked)

    def meta_copy(d):
        return remote(meta_ref, meta.at[z], meta_ssem.at[d], meta_rsem.at[d], at(y, (z + d) % RING))

    meta_local = pltpu.make_async_copy(meta_ref, meta.at[z], meta_rsem.at[0])
    meta_local.start()
    for d in (1, 7, 2, 6, 3, 5, 4):
        meta_copy(d).start()

    def down_copy(d):
        other = (q + d) % SPLIT
        return remote(
            wd_hbm.at[:, pl.ds(pl.multiple_of(other * cols, cols), cols)], wd.at[q],
            wd_ssem.at[d], wd_rsem.at[d], at(y, half * SPLIT + other),
        )

    row_id = lax.broadcasted_iota(jnp.int32, (RING, slot, 2 * tok), 1)
    dest_id = lax.broadcasted_iota(jnp.int32, (RING, slot, 2 * tok), 0)
    lane_id = lax.broadcasted_iota(jnp.int32, (RING, slot, 2 * tok), 2)
    row_odd = (row_id >= CAP).astype(jnp.int32)
    lane_odd = (lane_id >= tok).astype(jnp.int32)
    key = dest_id * slot + half * CAP + row_id - CAP * row_odd
    key = jnp.where(row_odd == lane_odd, key, -1).astype(jnp.float32).reshape(RING * slot, 2 * tok)
    odd_row = lax.broadcasted_iota(jnp.int32, (RING, slot, wg.shape[1]), 1).reshape(RING * slot, wg.shape[1]) >= CAP
    low_lane = lax.broadcasted_iota(jnp.int32, (1, 2 * tok), 1) < tok

    def step(st, carry):
        @pl.when(st == 1)
        def _():
            @pl.when(section == 0)
            def _():
                state[1] = incoming_ref[...]

            @pl.when(section > 0)
            def _():
                remote(out_ref, state.at[1], pass_ssem, pass_rsem, {"section": section}).wait_recv()

        x = state[st].astype(jnp.float32)
        scale = lax.rsqrt(jnp.mean(x * x, axis=-1, keepdims=True) + 1e-06)
        tokens[st, z] = (x * scale * gain_ref[...]).astype(jnp.bfloat16)

        def ring_copy(way, hop):
            sign = 1 - 2 * way
            block = tokens.at[st, (z - sign * (hop - 1) + RING) % RING]
            return remote(
                block, block, ring_ssem.at[way, hop - 1], ring_rsem.at[st, way, hop - 1], at(y, (z + sign + RING) % RING)
            )

        def hop(n):
            for way in range(2):
                if n < RING // 2 - 1:
                    ring_copy(way, n).wait_recv()
                    ring_copy(way, n + 1).start()
                elif n < RING // 2:
                    ring_copy(way, n).wait_recv()

                    @pl.when(par == 1 - way)
                    def _():
                        ring_copy(way, n + 1).start()
                else:
                    @pl.when(par == way)
                    def _():
                        ring_copy(way, n).wait_recv()

        def lanes(pair, row):
            return jnp.where(low_lane, meta[2 * pair, st, row : row + 1, :], meta[2 * pair + 1, st, row : row + 1, :])

        def row_copy(n, d):
            dest = (y + d) % RING
            return remote(sent.at[n, dest], rows.at[st, n, y], row_ssem.at[n, d], row_rsem.at[st, n, d], at(dest, z))

        def row_local(n):
            return pltpu.make_async_copy(sent.at[n, y], rows.at[st, n, y], row_rsem.at[st, n, 0])

        def select(n, pair):
            pick = ((key == lanes(pair, 0)) | (key == lanes(pair, 1))).astype(jnp.bfloat16)
            block = tokens[st, pl.ds(2 * pair, 2)].reshape(2 * tok, width)
            for c in range(0, width, 512):
                got = jnp.dot(pick, block[:, c : c + 512], preferred_element_type=jnp.float32)
                sent[n, :, :, c : c + 512] = got.astype(jnp.bfloat16).reshape(RING, slot, 512)
            for d in FAR_FIRST:
                row_copy(n, d).start()
            row_local(n).start()

        def one_place(i):
            return rows_one.at[st, (0, 0, 1, 2)[i], 1 - par if i == 1 else par]

        def one_copy(i, d):
            dest = (y + d) % RING
            return remote(
                sent_one.at[i, dest], one_place(i).at[y], one_ssem.at[i, d], one_rsem.at[st, i, d], at(dest, z)
            )

        def one_local(i):
            return pltpu.make_async_copy(sent_one.at[i, y], one_place(i).at[y], one_rsem.at[st, i, 0])

        def select_one(i, column):
            pick = (key == meta[column, st, 0:1, :]) | (key == meta[column, st, 1:2, :])
            block = jnp.concatenate([tokens[st, column, :, :span], tokens[st, column, :, span:]], axis=0)
            for c in range(0, span, 512):
                got = jnp.dot(pick.astype(jnp.bfloat16), block[:, c : c + 512], preferred_element_type=jnp.float32)
                sent_one[i, :, :, c : c + 512] = got.astype(jnp.bfloat16).reshape(RING, slot, 512)
            for d in FAR_FIRST:
                one_copy(i, d).start()
            one_local(i).start()

        def one_wait(i, d):
            if d == 0:
                one_local(i).wait()
            else:
                one_copy(i, d).wait_recv()

        def relay_copy(c, d, mine):
            place = rows_one.at[st, c, par if mine else 1 - par, (y - d + RING) % RING]
            return remote(place, place, relay_ssem.at[c - 1, d], relay_rsem.at[st, c - 1, d], at(y, mate))

        def relay(c):
            for d in (0,) + FAR_FIRST:
                one_wait(c + 1, d)
                relay_copy(c, d, True).start()

        def hidden_copy(pair, source, k, device):
            block = hidden.at[st, pair, source]
            return remote(block, block, hid_ssem.at[pair, k], hid_rsem.at[st, pair, source], at(y, half * SPLIT + device))

        def share(pair, gate, up):
            act = gate / (1.0 + jnp.exp(-gate)) * up
            hidden[st, pair, q] = act.astype(jnp.bfloat16)
            hidden_copy(pair, q, 0, other).start()
            hidden_copy(pair, q, 1, peer).start()
            hidden_copy(pair, q, 2, other_outer).start()

        def forward(n, pair):
            row_local(n).wait()
            for d in range(1, RING):
                row_copy(n, d).wait_recv()
            arrived = rows[st, n].reshape(RING * slot, width)
            gate = jnp.dot(arrived, wg[...], preferred_element_type=jnp.float32)
            up = jnp.dot(arrived, wu[...], preferred_element_type=jnp.float32)
            share(pair, gate, up)

        def forward_one(c, pair):
            for d in range(RING):
                if c == 0:
                    one_wait(0, d)
                    one_wait(1, d)
                else:
                    relay_copy(c, d, False).wait_recv()
            even = rows_one[st, c, 0].reshape(RING * slot, span)
            odd = rows_one[st, c, 1].reshape(RING * slot, span)

            def project(w):
                top, bottom = w[:span], w[span:]
                dot = lambda a, b: jnp.dot(a, b, preferred_element_type=jnp.float32)
                from_even = dot(even, top) + pltpu.roll(dot(even, bottom), RING * slot - CAP, 0)
                from_odd = pltpu.roll(dot(odd, top), CAP, 0) + dot(odd, bottom)
                return jnp.where(odd_row, from_odd, from_even)

            share(pair, project(wg), project(wu))

        def back_copy(pair, d):
            dest = (y + d) % RING
            return remote(
                back.at[pair, dest], returned.at[st, pair, y], back_ssem.at[pair, d], back_rsem.at[st, pair, d], at(dest, z)
            )

        def back_local(pair):
            return pltpu.make_async_copy(back.at[pair, y], returned.at[st, pair, y], back_rsem.at[st, pair, 0])

        def down(pair):
            hidden_copy(pair, peer, 0, q).wait_recv()
            for source in (other, other_outer):
                hidden_copy(pair, source, 0, q).wait_recv()
            total = jnp.dot(hidden[st, pair, 0], wd[0], preferred_element_type=jnp.float32)
            for k in range(1, SPLIT):
                total += jnp.dot(hidden[st, pair, k], wd[k], preferred_element_type=jnp.float32)
            back[pair] = total.astype(jnp.bfloat16).reshape(RING, slot, cols)
            for d in (4, 3, 5, 2, 6, 1, 7):
                back_copy(pair, d).start()
            back_local(pair).start()

        def part_copy(pair, b):
            dest = 2 * pair + b
            return remote(
                part.at[pair, b], parts.at[st, z], part_ssem.at[pair, b], part_rsem.at[st, (dest - z + RING) % RING], at(y, dest)
            )

        def part_local(pair, b):
            return pltpu.make_async_copy(part.at[pair, b], parts.at[st, z], part_rsem.at[st, 0])

        def combine(pair):
            back_local(pair).wait()
            for d in range(1, RING):
                back_copy(pair, d).wait_recv()
            mix = jnp.where(key == lanes(pair, 0), lanes(pair, 2), 0.0) + jnp.where(key == lanes(pair, 1), lanes(pair, 3), 0.0)
            high = mix.astype(jnp.bfloat16)
            low = (mix - high.astype(jnp.float32)).astype(jnp.bfloat16)
            values = returned[st, pair].reshape(RING * slot, cols)
            dims = (((0,), (0,)), ((), ()))
            total = lax.dot_general(high, values, dims, preferred_element_type=jnp.float32)
            total += lax.dot_general(low, values, dims, preferred_element_type=jnp.float32)
            part[pair] = total.astype(jnp.bfloat16).reshape(2, tok, cols)
            for b in range(2):
                @pl.when(2 * pair + b == z)
                def _():
                    part_local(pair, b).start()

                @pl.when(2 * pair + b != z)
                def _():
                    part_copy(pair, b).start()

        sibling, near, far = own + 1 - 2 * (own % 2), PAIRS - 1 - own, (own + 2) % PAIRS
        first, second = half * 2, half * 2 + 1
        third, fourth = (half * 2 + 2) % PAIRS, (half * 2 + 3) % PAIRS

        for way in range(2):
            ring_copy(way, 1).start()

        @pl.when(st == 0)
        def _():
            meta_local.wait()

        select_one(0, z)

        @pl.when(st == 0)
        def _():
            for d in (1, 7):
                meta_copy(d).wait_recv()

        hop(1)
        select_one(1, mate)

        @pl.when(st == 0)
        def _():
            for d in range(2, 7):
                meta_copy(d).wait_recv()

        hop(2)
        select_one(2, 2 * sibling + par)
        if NEAR_ONE:
            select_one(3, 2 * near + par)

        @pl.when(st == 0)
        def _():
            load_g.wait()
            load_u.wait()

        forward_one(0, own)
        hop(3)

        @pl.when(st == 0)
        def _():
            for d in range(1, SPLIT):
                down_copy(d).start()

        if not NEAR_ONE:
            select(0, near)
        relay(1)
        hop(4)
        select(1, far)

        if NEAR_ONE:
            relay(2)
        forward_one(1, sibling)
        if NEAR_ONE:
            forward_one(2, near)
        else:
            forward(0, near)

        @pl.when(st == 0)
        def _():
            load_d.wait()
            for d in range(1, SPLIT):
                down_copy(d).wait_recv()

        down(first)
        down(second)
        forward(1, far)
        combine(first)
        combine(second)
        down(third)
        down(fourth)
        combine(third)
        combine(fourth)

        part_own = pltpu.make_async_copy(part.at[0, 0], parts.at[st, z], part_rsem.at[st, 0])
        part_own.wait()
        for d in range(1, RING):
            remote(part.at[0, 0], parts.at[st, z], part_ssem.at[0, 0], part_rsem.at[st, d], at(y, z)).wait_recv()
        for k in range(SPLIT):
            block = slice(k * cols, (k + 1) * cols)
            total = parts[st, k].astype(jnp.float32) + parts[st, SPLIT + k].astype(jnp.float32)
            out_ref[:, block] = (state[st, :, block].astype(jnp.float32) + total).astype(jnp.bfloat16)

        pass_on = remote(out_ref, state.at[1], pass_ssem, pass_rsem, {"section": section + 1})

        @pl.when((st == 0) & (section < sections - 1))
        def _():
            pass_on.start()

        for way in range(2):
            for n in range(1, RING // 2):
                ring_copy(way, n).wait_send()

            @pl.when(par == 1 - way)
            def _():
                ring_copy(way, RING // 2).wait_send()

        for d in range(1, RING):
            for n in range(1 if NEAR_ONE else 0, 2):
                row_copy(n, d).wait_send()
            for i in range(4 if NEAR_ONE else 3):
                one_copy(i, d).wait_send()
        for c in range(1, 3 if NEAR_ONE else 2):
            for d in range(RING):
                relay_copy(c, d, True).wait_send()
        for pair in range(PAIRS):
            hidden_copy(pair, q, 0, other).wait_send()
            hidden_copy(pair, q, 1, peer).wait_send()
            hidden_copy(pair, q, 2, other_outer).wait_send()
        for pair in range(PAIRS):
            for d in range(1, RING):
                back_copy(pair, d).wait_send()
            for b in range(2):
                @pl.when(2 * pair + b != z)
                def _():
                    part_copy(pair, b).wait_send()

        @pl.when((st == 0) & (section < sections - 1))
        def _():
            pass_on.wait_send()

        return carry

    lax.fori_loop(0, STEPS, step, 0)
    for d in range(1, RING):
        meta_copy(d).wait_send()
    for d in range(1, SPLIT):
        down_copy(d).wait_send()


def on_device(carried, incoming, norm_gain, expert_ids, gate_weights, w_gate, w_up, w_down):
    ids, gates = jnp.swapaxes(expert_ids[0], 1, 2), jnp.swapaxes(gate_weights[0], 1, 2)
    tok, width = carried.shape[1:]
    units = w_gate.shape[2]
    cols = width // SPLIT
    slot = 2 * CAP
    lanes = 2 * tok
    bf16 = jnp.bfloat16
    dma = pltpu.SemaphoreType.DMA
    vmem = pl.BlockSpec(memory_space=pltpu.VMEM)
    hbm = pl.BlockSpec(memory_space=pl.ANY)
    out = pl.pallas_call(
        kernel,
        out_shape=jax.ShapeDtypeStruct((tok, width), bf16),
        in_specs=[vmem] * 5 + [hbm] * 3,
        out_specs=vmem,
        scratch_shapes=[
            pltpu.VMEM((STEPS, tok, width), bf16),
            pltpu.VMEM((STEPS, RING, tok, width), bf16),
            pltpu.VMEM((STEPS, 8, lanes), jnp.float32),
            pltpu.VMEM((RING, STEPS, 8, lanes), jnp.float32),
            pltpu.VMEM((2, RING, slot, width), bf16),
            pltpu.VMEM((STEPS, 2, RING, slot, width), bf16),
            pltpu.VMEM((4, RING, slot, width // 2), bf16),
            pltpu.VMEM((STEPS, 3, 2, RING, slot, width // 2), bf16),
            pltpu.VMEM((STEPS, PAIRS, SPLIT, RING * slot, units), bf16),
            pltpu.VMEM((PAIRS, RING, slot, cols), bf16),
            pltpu.VMEM((STEPS, PAIRS, RING, slot, cols), bf16),
            pltpu.VMEM((PAIRS, 2, tok, cols), bf16),
            pltpu.VMEM((STEPS, RING, tok, cols), bf16),
            pltpu.VMEM((width, units), bf16),
            pltpu.VMEM((width, units), bf16),
            pltpu.VMEM((SPLIT, units, cols), bf16),
            dma((3,)), dma((RING,)), dma((RING,)), dma((SPLIT,)), dma((SPLIT,)),
            dma((2, 4)), dma((STEPS, 2, 4)),
            dma((2, RING)), dma((STEPS, 2, RING)),
            dma((4, RING)), dma((STEPS, 4, RING)),
            dma((2, RING)), dma((STEPS, 2, RING)),
            dma((PAIRS, SPLIT)), dma((STEPS, PAIRS, SPLIT)),
            dma((PAIRS, RING)), dma((STEPS, PAIRS, RING)),
            dma((PAIRS, 2)), dma((STEPS, RING)),
            dma, dma,
        ],
        compiler_params=pltpu.CompilerParams(
            collective_id=0, has_side_effects=True, vmem_limit_bytes=62 * 1024 * 1024
        ),
    )(carried[0], incoming[0], norm_gain, ids, gates, w_gate[0], w_up[0], w_down[0])
    return out[None]


def solution(mesh):
    return jax.shard_map(
        on_device,
        mesh=mesh,
        in_specs=(
            P("section", "expert", None),
            P(None, "expert", None),
            P("section", None),
            P("section", None, "expert", None),
            P("section", None, "expert", None),
            P("section", None, "expert"),
            P("section", None, "expert"),
            P("section", "expert", None),
        ),
        out_specs=P("section", "expert", None),
        check_vma=False,
    )
```

```python
import jax
import jax.numpy as jnp
from jax import lax
from jax.experimental import pallas as pl
from jax.experimental.pallas import tpu as pltpu
from jax.sharding import PartitionSpec as P

EXPERTS = 16
TOP = 2
STEPS = 2
CAP = 12
SPLIT = 4
RING = 8
PAIRS = RING // 2
MESH = pl.DeviceIdType.MESH
NEAR_ONE = True
NEAR_FIRST = (1, 7, 2, 6, 3, 5, 4)


def routing(st, ids_ref, gates_ref, meta_ref):
    twice = lambda row: jnp.concatenate([row, row], axis=1)
    tok = ids_ref.shape[2]
    first, second = twice(ids_ref[st, 0:1, :]), twice(ids_ref[st, 1:2, :])
    expert = lax.broadcasted_iota(jnp.int32, (EXPERTS, 2 * tok), 0)
    lane = lax.broadcasted_iota(jnp.int32, (2 * tok, 2 * tok), 1)
    ahead = lax.broadcasted_iota(jnp.int32, (2 * tok, 2 * tok), 0) < lane - jnp.where(lane >= tok, tok, 0)
    ahead = ahead.astype(jnp.bfloat16)
    in_first = (expert == first).astype(jnp.float32)
    in_second = (expert == second).astype(jnp.float32)
    count = lambda hot: jnp.dot(hot.astype(jnp.bfloat16), ahead, preferred_element_type=jnp.float32)
    total = 0.5 * jnp.sum(in_first, axis=1, keepdims=True)
    place_first = jnp.sum(in_first * count(in_first), axis=0, keepdims=True)
    place_second = jnp.sum(in_second * (count(in_second) + total), axis=0, keepdims=True)
    meta_ref[st, 0:1, :] = first.astype(jnp.float32) * CAP + place_first
    meta_ref[st, 1:2, :] = second.astype(jnp.float32) * CAP + place_second
    meta_ref[st, 2:3, :] = twice(gates_ref[st, 0:1, :])
    meta_ref[st, 3:4, :] = twice(gates_ref[st, 1:2, :])
    meta_ref[st, 4:8, :] = jnp.zeros((4, 2 * tok), jnp.float32)


def kernel(
    carried_ref, incoming_ref, gain_ref, ids_ref, gates_ref, wg_hbm, wu_hbm, wd_hbm,
    out_ref,
    state, tokens, meta_ref, meta, sent, rows, sent_one, rows_one, hidden, back, returned, part, parts, wg, wu, wd,
    w_sem, meta_ssem, meta_rsem, wd_ssem, wd_rsem,
    ring_ssem, ring_rsem, row_ssem, row_rsem, one_ssem, one_rsem, relay_ssem, relay_rsem, hid_ssem, hid_rsem,
    back_ssem, back_rsem, part_ssem, part_rsem, pass_ssem, pass_rsem,
):
    section = lax.axis_index("section")
    sections = lax.axis_size("section")
    me = lax.axis_index("expert")
    y, z = me // RING, me % RING
    half, q = z // SPLIT, z % SPLIT
    own = z // 2
    par = z % 2
    mate = z + 1 - 2 * par
    peer = q + 1 - 2 * par
    other = 2 - q // 2
    other_outer = 3 - 3 * (q // 2)
    tok = carried_ref.shape[0]
    width = carried_ref.shape[1]
    slot = 2 * CAP
    cols = wd.shape[2]
    span = width // 2

    def at(yy, zz):
        return {"expert": yy * RING + zz}

    def remote(src, dst, ssem, rsem, device):
        return pltpu.make_async_remote_copy(
            src_ref=src, dst_ref=dst, send_sem=ssem, recv_sem=rsem, device_id=device, device_id_type=MESH
        )

    load_g = pltpu.make_async_copy(wg_hbm, wg, w_sem.at[0])
    load_u = pltpu.make_async_copy(wu_hbm, wu, w_sem.at[1])
    load_d = pltpu.make_async_copy(wd_hbm.at[:, pl.ds(pl.multiple_of(q * cols, cols), cols)], wd.at[q], w_sem.at[2])
    load_g.start()
    load_u.start()
    load_d.start()

    barrier = pltpu.get_barrier_semaphore()
    for d in range(1, RING):
        pl.semaphore_signal(barrier, inc=1, device_id=at(y, (z + d) % RING), device_id_type=MESH)
        pl.semaphore_signal(barrier, inc=1, device_id=at((y + d) % RING, z), device_id_type=MESH)

    @pl.when(section > 0)
    def _():
        pl.semaphore_signal(barrier, inc=1, device_id={"section": section - 1}, device_id_type=MESH)

    @pl.when(section < sections - 1)
    def _():
        pl.semaphore_signal(barrier, inc=1, device_id={"section": section + 1}, device_id_type=MESH)

    state[0] = carried_ref[...]
    for st in range(STEPS):
        routing(st, ids_ref, gates_ref, meta_ref)
    linked = (section > 0).astype(jnp.int32) + (section < sections - 1).astype(jnp.int32)
    pl.semaphore_wait(barrier, 2 * (RING - 1) + linked)

    def meta_copy(d):
        return remote(meta_ref, meta.at[z], meta_ssem.at[d], meta_rsem.at[d], at(y, (z + d) % RING))

    meta_local = pltpu.make_async_copy(meta_ref, meta.at[z], meta_rsem.at[0])
    meta_local.start()
    for d in (1, 7, 2, 6, 3, 5, 4):
        meta_copy(d).start()

    def down_copy(d):
        other = (q + d) % SPLIT
        return remote(
            wd_hbm.at[:, pl.ds(pl.multiple_of(other * cols, cols), cols)], wd.at[q],
            wd_ssem.at[d], wd_rsem.at[d], at(y, half * SPLIT + other),
        )

    row_id = lax.broadcasted_iota(jnp.int32, (RING, slot, 2 * tok), 1)
    dest_id = lax.broadcasted_iota(jnp.int32, (RING, slot, 2 * tok), 0)
    lane_id = lax.broadcasted_iota(jnp.int32, (RING, slot, 2 * tok), 2)
    row_odd = (row_id >= CAP).astype(jnp.int32)
    lane_odd = (lane_id >= tok).astype(jnp.int32)
    key = dest_id * slot + half * CAP + row_id - CAP * row_odd
    key = jnp.where(row_odd == lane_odd, key, -1).astype(jnp.float32).reshape(RING * slot, 2 * tok)
    odd_row = lax.broadcasted_iota(jnp.int32, (RING, slot, wg.shape[1]), 1).reshape(RING * slot, wg.shape[1]) >= CAP
    low_lane = lax.broadcasted_iota(jnp.int32, (1, 2 * tok), 1) < tok

    def step(st, carry):
        @pl.when(st == 1)
        def _():
            @pl.when(section == 0)
            def _():
                state[1] = incoming_ref[...]

            @pl.when(section > 0)
            def _():
                remote(out_ref, state.at[1], pass_ssem, pass_rsem, {"section": section}).wait_recv()

        x = state[st].astype(jnp.float32)
        scale = lax.rsqrt(jnp.mean(x * x, axis=-1, keepdims=True) + 1e-06)
        tokens[st, z] = (x * scale * gain_ref[...]).astype(jnp.bfloat16)

        def ring_copy(way, hop):
            sign = 1 - 2 * way
            block = tokens.at[st, (z - sign * (hop - 1) + RING) % RING]
            return remote(
                block, block, ring_ssem.at[way, hop - 1], ring_rsem.at[st, way, hop - 1], at(y, (z + sign + RING) % RING)
            )

        def hop(n):
            for way in range(2):
                if n < RING // 2 - 1:
                    ring_copy(way, n).wait_recv()
                    ring_copy(way, n + 1).start()
                elif n < RING // 2:
                    ring_copy(way, n).wait_recv()

                    @pl.when(par == 1 - way)
                    def _():
                        ring_copy(way, n + 1).start()
                else:
                    @pl.when(par == way)
                    def _():
                        ring_copy(way, n).wait_recv()

        def lanes(pair, row):
            return jnp.where(low_lane, meta[2 * pair, st, row : row + 1, :], meta[2 * pair + 1, st, row : row + 1, :])

        def row_copy(n, d):
            dest = (y + d) % RING
            return remote(sent.at[n, dest], rows.at[st, n, y], row_ssem.at[n, d], row_rsem.at[st, n, d], at(dest, z))

        def row_local(n):
            return pltpu.make_async_copy(sent.at[n, y], rows.at[st, n, y], row_rsem.at[st, n, 0])

        def select(n, pair):
            pick = ((key == lanes(pair, 0)) | (key == lanes(pair, 1))).astype(jnp.bfloat16)
            block = tokens[st, pl.ds(2 * pair, 2)].reshape(2 * tok, width)
            for c in range(0, width, 512):
                got = jnp.dot(pick, block[:, c : c + 512], preferred_element_type=jnp.float32)
                sent[n, :, :, c : c + 512] = got.astype(jnp.bfloat16).reshape(RING, slot, 512)
            for d in NEAR_FIRST:
                row_copy(n, d).start()
            row_local(n).start()

        def one_place(i):
            return rows_one.at[st, (0, 0, 1, 2)[i], 1 - par if i == 1 else par]

        def one_copy(i, d):
            dest = (y + d) % RING
            return remote(
                sent_one.at[i, dest], one_place(i).at[y], one_ssem.at[i, d], one_rsem.at[st, i, d], at(dest, z)
            )

        def one_local(i):
            return pltpu.make_async_copy(sent_one.at[i, y], one_place(i).at[y], one_rsem.at[st, i, 0])

        def select_one(i, column):
            pick = (key == meta[column, st, 0:1, :]) | (key == meta[column, st, 1:2, :])
            block = jnp.concatenate([tokens[st, column, :, :span], tokens[st, column, :, span:]], axis=0)
            for c in range(0, span, 512):
                got = jnp.dot(pick.astype(jnp.bfloat16), block[:, c : c + 512], preferred_element_type=jnp.float32)
                sent_one[i, :, :, c : c + 512] = got.astype(jnp.bfloat16).reshape(RING, slot, 512)
            for d in NEAR_FIRST:
                one_copy(i, d).start()
            one_local(i).start()

        def one_wait(i, d):
            if d == 0:
                one_local(i).wait()
            else:
                one_copy(i, d).wait_recv()

        def relay_copy(c, d, mine):
            place = rows_one.at[st, c, par if mine else 1 - par, (y - d + RING) % RING]
            return remote(place, place, relay_ssem.at[c - 1, d], relay_rsem.at[st, c - 1, d], at(y, mate))

        def relay(c):
            for d in (0,) + NEAR_FIRST:
                one_wait(c + 1, d)
                relay_copy(c, d, True).start()

        def hidden_copy(pair, source, k, device):
            block = hidden.at[st, pair, source]
            return remote(block, block, hid_ssem.at[pair, k], hid_rsem.at[st, pair, source], at(y, half * SPLIT + device))

        def share(pair, gate, up):
            act = gate / (1.0 + jnp.exp(-gate)) * up
            hidden[st, pair, q] = act.astype(jnp.bfloat16)
            hidden_copy(pair, q, 0, other).start()
            hidden_copy(pair, q, 1, peer).start()
            hidden_copy(pair, q, 2, other_outer).start()

        def forward(n, pair):
            row_local(n).wait()
            for d in range(1, RING):
                row_copy(n, d).wait_recv()
            arrived = rows[st, n].reshape(RING * slot, width)
            gate = jnp.dot(arrived, wg[...], preferred_element_type=jnp.float32)
            up = jnp.dot(arrived, wu[...], preferred_element_type=jnp.float32)
            share(pair, gate, up)

        def forward_one(c, pair):
            for d in range(RING):
                if c == 0:
                    one_wait(0, d)
                    one_wait(1, d)
                else:
                    relay_copy(c, d, False).wait_recv()
            even = rows_one[st, c, 0].reshape(RING * slot, span)
            odd = rows_one[st, c, 1].reshape(RING * slot, span)

            def project(w):
                top, bottom = w[:span], w[span:]
                dot = lambda a, b: jnp.dot(a, b, preferred_element_type=jnp.float32)
                from_even = dot(even, top) + pltpu.roll(dot(even, bottom), RING * slot - CAP, 0)
                from_odd = pltpu.roll(dot(odd, top), CAP, 0) + dot(odd, bottom)
                return jnp.where(odd_row, from_odd, from_even)

            share(pair, project(wg), project(wu))

        def back_copy(pair, d):
            dest = (y + d) % RING
            return remote(
                back.at[pair, dest], returned.at[st, pair, y], back_ssem.at[pair, d], back_rsem.at[st, pair, d], at(dest, z)
            )

        def back_local(pair):
            return pltpu.make_async_copy(back.at[pair, y], returned.at[st, pair, y], back_rsem.at[st, pair, 0])

        def down(pair):
            hidden_copy(pair, peer, 0, q).wait_recv()
            for source in (other, other_outer):
                hidden_copy(pair, source, 0, q).wait_recv()
            total = jnp.dot(hidden[st, pair, 0], wd[0], preferred_element_type=jnp.float32)
            for k in range(1, SPLIT):
                total += jnp.dot(hidden[st, pair, k], wd[k], preferred_element_type=jnp.float32)
            back[pair] = total.astype(jnp.bfloat16).reshape(RING, slot, cols)
            for d in (4, 3, 5, 2, 6, 1, 7):
                back_copy(pair, d).start()
            back_local(pair).start()

        def part_copy(pair, b):
            dest = 2 * pair + b
            return remote(
                part.at[pair, b], parts.at[st, z], part_ssem.at[pair, b], part_rsem.at[st, (dest - z + RING) % RING], at(y, dest)
            )

        def part_local(pair, b):
            return pltpu.make_async_copy(part.at[pair, b], parts.at[st, z], part_rsem.at[st, 0])

        def combine(pair):
            back_local(pair).wait()
            for d in range(1, RING):
                back_copy(pair, d).wait_recv()
            mix = jnp.where(key == lanes(pair, 0), lanes(pair, 2), 0.0) + jnp.where(key == lanes(pair, 1), lanes(pair, 3), 0.0)
            high = mix.astype(jnp.bfloat16)
            low = (mix - high.astype(jnp.float32)).astype(jnp.bfloat16)
            values = returned[st, pair].reshape(RING * slot, cols)
            dims = (((0,), (0,)), ((), ()))
            total = lax.dot_general(high, values, dims, preferred_element_type=jnp.float32)
            total += lax.dot_general(low, values, dims, preferred_element_type=jnp.float32)
            part[pair] = total.astype(jnp.bfloat16).reshape(2, tok, cols)
            for b in range(2):
                @pl.when(2 * pair + b == z)
                def _():
                    part_local(pair, b).start()

                @pl.when(2 * pair + b != z)
                def _():
                    part_copy(pair, b).start()

        sibling, near, far = own + 1 - 2 * (own % 2), PAIRS - 1 - own, (own + 2) % PAIRS
        first, second = half * 2, half * 2 + 1
        third, fourth = (half * 2 + 2) % PAIRS, (half * 2 + 3) % PAIRS

        for way in range(2):
            ring_copy(way, 1).start()

        @pl.when(st == 0)
        def _():
            meta_local.wait()

        select_one(0, z)

        @pl.when(st == 0)
        def _():
            for d in (1, 7):
                meta_copy(d).wait_recv()

        hop(1)
        select_one(1, mate)

        @pl.when(st == 0)
        def _():
            for d in range(2, 7):
                meta_copy(d).wait_recv()

        hop(2)
        select_one(2, 2 * sibling + par)
        if NEAR_ONE:
            select_one(3, 2 * near + par)

        @pl.when(st == 0)
        def _():
            load_g.wait()
            load_u.wait()

        forward_one(0, own)
        hop(3)

        @pl.when(st == 0)
        def _():
            for d in range(1, SPLIT):
                down_copy(d).start()

        if not NEAR_ONE:
            select(0, near)
        relay(1)
        hop(4)
        select(1, far)

        if NEAR_ONE:
            relay(2)
        forward_one(1, sibling)
        if NEAR_ONE:
            forward_one(2, near)
        else:
            forward(0, near)

        @pl.when(st == 0)
        def _():
            load_d.wait()
            for d in range(1, SPLIT):
                down_copy(d).wait_recv()

        down(first)
        down(second)
        forward(1, far)
        combine(first)
        combine(second)
        down(third)
        down(fourth)
        combine(third)
        combine(fourth)

        part_own = pltpu.make_async_copy(part.at[0, 0], parts.at[st, z], part_rsem.at[st, 0])
        part_own.wait()
        for d in range(1, RING):
            remote(part.at[0, 0], parts.at[st, z], part_ssem.at[0, 0], part_rsem.at[st, d], at(y, z)).wait_recv()
        for k in range(SPLIT):
            block = slice(k * cols, (k + 1) * cols)
            total = parts[st, k].astype(jnp.float32) + parts[st, SPLIT + k].astype(jnp.float32)
            out_ref[:, block] = (state[st, :, block].astype(jnp.float32) + total).astype(jnp.bfloat16)

        pass_on = remote(out_ref, state.at[1], pass_ssem, pass_rsem, {"section": section + 1})

        @pl.when((st == 0) & (section < sections - 1))
        def _():
            pass_on.start()

        for way in range(2):
            for n in range(1, RING // 2):
                ring_copy(way, n).wait_send()

            @pl.when(par == 1 - way)
            def _():
                ring_copy(way, RING // 2).wait_send()

        for d in range(1, RING):
            for n in range(1 if NEAR_ONE else 0, 2):
                row_copy(n, d).wait_send()
            for i in range(4 if NEAR_ONE else 3):
                one_copy(i, d).wait_send()
        for c in range(1, 3 if NEAR_ONE else 2):
            for d in range(RING):
                relay_copy(c, d, True).wait_send()
        for pair in range(PAIRS):
            hidden_copy(pair, q, 0, other).wait_send()
            hidden_copy(pair, q, 1, peer).wait_send()
            hidden_copy(pair, q, 2, other_outer).wait_send()
        for pair in range(PAIRS):
            for d in range(1, RING):
                back_copy(pair, d).wait_send()
            for b in range(2):
                @pl.when(2 * pair + b != z)
                def _():
                    part_copy(pair, b).wait_send()

        @pl.when((st == 0) & (section < sections - 1))
        def _():
            pass_on.wait_send()

        return carry

    lax.fori_loop(0, STEPS, step, 0)
    for d in range(1, RING):
        meta_copy(d).wait_send()
    for d in range(1, SPLIT):
        down_copy(d).wait_send()


def on_device(carried, incoming, norm_gain, expert_ids, gate_weights, w_gate, w_up, w_down):
    ids, gates = jnp.swapaxes(expert_ids[0], 1, 2), jnp.swapaxes(gate_weights[0], 1, 2)
    tok, width = carried.shape[1:]
    units = w_gate.shape[2]
    cols = width // SPLIT
    slot = 2 * CAP
    lanes = 2 * tok
    bf16 = jnp.bfloat16
    dma = pltpu.SemaphoreType.DMA
    vmem = pl.BlockSpec(memory_space=pltpu.VMEM)
    hbm = pl.BlockSpec(memory_space=pl.ANY)
    out = pl.pallas_call(
        kernel,
        out_shape=jax.ShapeDtypeStruct((tok, width), bf16),
        in_specs=[vmem] * 5 + [hbm] * 3,
        out_specs=vmem,
        scratch_shapes=[
            pltpu.VMEM((STEPS, tok, width), bf16),
            pltpu.VMEM((STEPS, RING, tok, width), bf16),
            pltpu.VMEM((STEPS, 8, lanes), jnp.float32),
            pltpu.VMEM((RING, STEPS, 8, lanes), jnp.float32),
            pltpu.VMEM((2, RING, slot, width), bf16),
            pltpu.VMEM((STEPS, 2, RING, slot, width), bf16),
            pltpu.VMEM((4, RING, slot, width // 2), bf16),
            pltpu.VMEM((STEPS, 3, 2, RING, slot, width // 2), bf16),
            pltpu.VMEM((STEPS, PAIRS, SPLIT, RING * slot, units), bf16),
            pltpu.VMEM((PAIRS, RING, slot, cols), bf16),
            pltpu.VMEM((STEPS, PAIRS, RING, slot, cols), bf16),
            pltpu.VMEM((PAIRS, 2, tok, cols), bf16),
            pltpu.VMEM((STEPS, RING, tok, cols), bf16),
            pltpu.VMEM((width, units), bf16),
            pltpu.VMEM((width, units), bf16),
            pltpu.VMEM((SPLIT, units, cols), bf16),
            dma((3,)), dma((RING,)), dma((RING,)), dma((SPLIT,)), dma((SPLIT,)),
            dma((2, 4)), dma((STEPS, 2, 4)),
            dma((2, RING)), dma((STEPS, 2, RING)),
            dma((4, RING)), dma((STEPS, 4, RING)),
            dma((2, RING)), dma((STEPS, 2, RING)),
            dma((PAIRS, SPLIT)), dma((STEPS, PAIRS, SPLIT)),
            dma((PAIRS, RING)), dma((STEPS, PAIRS, RING)),
            dma((PAIRS, 2)), dma((STEPS, RING)),
            dma, dma,
        ],
        compiler_params=pltpu.CompilerParams(
            collective_id=0, has_side_effects=True, vmem_limit_bytes=62 * 1024 * 1024
        ),
    )(carried[0], incoming[0], norm_gain, ids, gates, w_gate[0], w_up[0], w_down[0])
    return out[None]


def solution(mesh):
    return jax.shard_map(
        on_device,
        mesh=mesh,
        in_specs=(
            P("section", "expert", None),
            P(None, "expert", None),
            P("section", None),
            P("section", None, "expert", None),
            P("section", None, "expert", None),
            P("section", None, "expert"),
            P("section", None, "expert"),
            P("section", "expert", None),
        ),
        out_specs=P("section", "expert", None),
        check_vma=False,
    )
```
